32 devices in a mesh: row: 2 (over x), col: 4 (over y, core), dp: 4 (over z).
Axes of the slice: x: 2, y: 2, z: 4, core: 2. Of those that a mesh axis runs over, the one named last changes fastest.
Arguments:
- tokens: bfloat16 [8192, 1152], P('dp', 'col'), may hold values from -6 to 6
- positions: int32 [8192], P('dp'), may hold values from 0 to 1023, as said below
- prefix: int32 [8], replicated, may hold values from 102 to 512
- norm1_gain: bfloat16 [1152], P(('col', 'dp')), may hold values from 0.5 to 1.5
- query_key_value_weight: bfloat16 [1152, 1920], P(('col', 'dp'), 'row'), may hold values from -0.1875 to 0.1875
- out_weight: bfloat16 [1152, 1152], P('row', ('col', 'dp')), may hold values from -2 to 2
- norm2_gain: bfloat16 [1152], P(('col', 'dp')), may hold values from 0.5 to 1.5
- gate_up_weight: bfloat16 [1152, 6144], P(('col', 'dp'), 'row'), may hold values from -0.1875 to 0.1875
- down_weight: bfloat16 [3072, 1152], P('row', ('col', 'dp')), may hold values from -0.109375 to 0.109375
- cotangent: bfloat16 [8192, 1152], P('dp', 'col'), may hold values from -6 to 6
Outputs:
- output: bfloat16 [8192, 1152], P('dp', 'col')
- input_grad: float32 [8192, 1152], P('dp', 'col')
- norm1_grad: float32 [1152], P(('col', 'dp'))
- qkv_grad: float32 [1152, 1920], P(('col', 'dp'), 'row')
- out_grad: float32 [1152, 1152], P('row', ('col', 'dp'))
- norm2_grad: float32 [1152], P(('col', 'dp'))
- gate_up_grad: float32 [1152, 6144], P(('col', 'dp'), 'row')
- down_grad: float32 [3072, 1152], P('row', ('col', 'dp'))
The draws below stay inside these ranges and needn't reach their ends.
Inputs may be any that keep to these rules, and one draw needn't show every extreme that they name: `positions`: within each sequence every place 0 to 1023 occurs once; the 256 rows of one sequence on one index of dp hold 256 consecutive places in increasing order, starting at a multiple of 256.
All inputs are finite; a program needn't handle non-finite values.
Results may differ from the reference program's by a relative error of at most 0.034.
Values may be sent and summed in bfloat16 or wider, within the bound.
A program may use at most 192 MiB of HBM per device.

```python
import jax
import jax.numpy as jnp
from jax import lax

MODEL_WIDTH = 1152
QUERY_HEADS = 18
KEY_VALUE_HEADS = 6
HEAD_SIZE = 64
FF = 3072
SEG = 256
SEQ_MB = 2
MB = 4
LEN = 1024
SEQS = 8
TOKENS = 8192
N_ROW = 2
N_DP = 4


def draw_positions(key, part):
    segments = LEN // SEG
    subkeys = jax.random.split(key, MB * SEQ_MB)

    def one_order(single):
        return jax.random.permutation(single, segments)
    orders = jax.vmap(one_order)(subkeys)
    starts = orders.T.reshape(segments, MB, SEQ_MB, 1) * SEG
    offsets = jnp.arange(SEG, dtype=jnp.int32).reshape(1, 1, 1, SEG)
    return (starts + offsets).reshape(segments * MB * SEQ_MB * SEG).astype(jnp.int32)


def touch_ends(entries, key, smallest, largest):
    extent = entries.shape
    index_at = [jax.random.randint(jax.random.fold_in(key, axis), (), 0, extent[axis]) for axis in range(len(extent))]
    entries = entries.at[tuple(index_at)].set(smallest)
    longest = extent.index(max(extent))
    index_at[longest] = (index_at[longest] + 1) % extent[longest]
    return entries.at[tuple(index_at)].set(largest)


def shard_levels(key, extent, cuts, least, high):
    level = 1.0
    for position, parts in cuts:
        heights = jax.random.uniform(jax.random.fold_in(jax.random.fold_in(key, 6), position), (parts,), jnp.float32, least / len(cuts), high / len(cuts))
        level = level * jnp.repeat(jnp.exp(heights), extent[position] // parts).reshape((-1,) + (1,) * (len(extent) - 1 - position))
    return level


def centred(rng, dims, width, most, cuts=(), held_as=jnp.bfloat16):
    values = width * jax.random.normal(rng, dims, jnp.float32)
    if cuts:
        values = values * shard_levels(rng, dims, cuts, -0.22, 0.18)
    return jnp.clip(values, -most, most).astype(held_as)


def setup_inputs(seed: int = 0) -> dict:
    key_of = jax.random.split(jax.random.key(seed), 11)
    tokens = centred(key_of[0], (TOKENS, MODEL_WIDTH), 1.0, 6.0, ((0, 4), (1, 4)))
    positions = draw_positions(jax.random.fold_in(key_of[10], 71), 0)
    prefix = touch_ends(jax.random.randint(key_of[2], (SEQS,), LEN // 10, LEN // 2 + 1), jax.random.fold_in(key_of[2], 1), LEN // 10, (LEN // 2 + 1) - 1).astype(jnp.int32)
    norm1_gain = jnp.clip(1.0 + 0.1 * jax.random.normal(key_of[3], (MODEL_WIDTH,), jnp.float32), 0.5, 1.5).astype(jnp.bfloat16)
    query_key_value_weight = centred(key_of[4], (MODEL_WIDTH, (QUERY_HEADS + 2 * KEY_VALUE_HEADS) * HEAD_SIZE), MODEL_WIDTH ** -0.5, 0.1875, ((0, 16), (1, 2)))
    out_weight = centred(key_of[5], (QUERY_HEADS * HEAD_SIZE, MODEL_WIDTH), (max(QUERY_HEADS * HEAD_SIZE // 128, 1)) ** -0.5, 2.0, ((0, 2), (1, 16)))
    norm2_gain = jnp.clip(1.0 + 0.1 * jax.random.normal(key_of[6], (MODEL_WIDTH,), jnp.float32), 0.5, 1.5).astype(jnp.bfloat16)
    gate_up_weight = centred(key_of[7], (MODEL_WIDTH, 2 * FF), MODEL_WIDTH ** -0.5, 0.1875, ((0, 16), (1, 2)))
    down_weight = centred(key_of[8], (FF, MODEL_WIDTH), FF ** -0.5, 0.109375, ((0, 2), (1, 16)))
    cotangent = centred(key_of[9], (TOKENS, MODEL_WIDTH), 1.0, 6.0, ((0, 4), (1, 4)))
    return dict(tokens=tokens, positions=positions, prefix=prefix, norm1_gain=norm1_gain, query_key_value_weight=query_key_value_weight, out_weight=out_weight, norm2_gain=norm2_gain, gate_up_weight=gate_up_weight, down_weight=down_weight, cotangent=cotangent)


@jax.custom_vjp
def low(v):
    return lax.optimization_barrier(v.astype(jnp.bfloat16)).astype(jnp.float32)

@jax.custom_vjp
def low_back(v):
    return v

def low_keep(v):
    return (low(v), None)

def low_pass(kept, grad):
    return (grad,)

def back_keep(v):
    return (v, None)

def back_low(kept, grad):
    return (low(grad),)
low.defvjp(low_keep, low_pass)
low_back.defvjp(back_keep, back_low)
EPSILON = 1e-05
THETA = 10000.0
MASKED = -1e+30
HIGHEST = lax.Precision.HIGHEST

def rope_tables(places):
    halfway = HEAD_SIZE // 2
    inverse = THETA ** (-(jnp.arange(halfway, dtype=jnp.float32) * 2.0 / HEAD_SIZE))
    angles = places.astype(jnp.float32)[:, None] * inverse[None, :]
    cosine = jnp.cos(angles)
    sine = jnp.sin(angles)
    return (jnp.concatenate([cosine, cosine], axis=-1), jnp.concatenate([sine, sine], axis=-1))

def turned(values):
    halfway = values.shape[-1] // 2
    return jnp.concatenate([-values[..., halfway:], values[..., :halfway]], axis=-1)

def rotate(values, cosine, sine):
    return values * cosine[:, None, :] + turned(values) * sine[:, None, :]

def rms_norm(values, gain):
    return values * lax.rsqrt(lax.optimization_barrier(jnp.mean(values * values, axis=-1, keepdims=True)) + EPSILON) * gain

def attention(queries, keys, values, places, limit):
    query_group = QUERY_HEADS // KEY_VALUE_HEADS
    keys_wide = jnp.repeat(keys, query_group, axis=1)
    values_wide = jnp.repeat(values, query_group, axis=1)
    sequence_length = queries.shape[0]
    block = 512 if sequence_length % 512 == 0 else sequence_length
    count = sequence_length // block

    def one_block(pair):
        query_block, query_places = pair
        scores = jnp.einsum('qhd,khd->hqk', query_block, keys_wide, precision=HIGHEST) * HEAD_SIZE ** (-0.5)
        scores = low_back(scores)
        allowed = (places[None, :] <= query_places[:, None]) | (places[None, :] < limit)
        scores = jnp.where(allowed[None], scores, MASKED)
        probs = jax.nn.softmax(scores, axis=-1)
        return jnp.einsum('hqk,khd->qhd', low(probs), values_wide, precision=HIGHEST)
    result = lax.map(jax.checkpoint(one_block), (queries.reshape(count, block, QUERY_HEADS, HEAD_SIZE), places.reshape(count, block)))
    return result.reshape(sequence_length, QUERY_HEADS, HEAD_SIZE)

def layer(inputs, gain_one, qkv_full, out_full, gain_two, gate_up_full, down_full, places, limit):
    sequence_length = inputs.shape[0]
    query_head_count = QUERY_HEADS // N_ROW
    key_value_heads = KEY_VALUE_HEADS // N_ROW
    normed_one = low(rms_norm(inputs, gain_one))
    mixed = low_back(jnp.dot(normed_one, qkv_full, precision=HIGHEST))
    group_count = mixed.reshape(sequence_length, N_ROW, (query_head_count + 2 * key_value_heads) * HEAD_SIZE)
    query_raw = group_count[:, :, :query_head_count * HEAD_SIZE].reshape(sequence_length, QUERY_HEADS, HEAD_SIZE)
    key_unrotated = group_count[:, :, query_head_count * HEAD_SIZE:(query_head_count + key_value_heads) * HEAD_SIZE].reshape(sequence_length, KEY_VALUE_HEADS, HEAD_SIZE)
    value_unshaped = group_count[:, :, (query_head_count + key_value_heads) * HEAD_SIZE:].reshape(sequence_length, KEY_VALUE_HEADS, HEAD_SIZE)
    cosine, sine = rope_tables(places)
    queries = low(rotate(query_raw, cosine, sine))
    keys = low(rotate(key_unrotated, cosine, sine))
    values = low(value_unshaped)
    heads = attention(queries, keys, values, places, limit).reshape(sequence_length, QUERY_HEADS * HEAD_SIZE)
    heads = low_back(low(heads))
    middle = inputs + low_back(jnp.dot(heads, out_full, precision=HIGHEST))
    normed_two = low(rms_norm(middle, gain_two))
    gate_up = low_back(jnp.dot(normed_two, gate_up_full, precision=HIGHEST))
    gate_up = gate_up.reshape(sequence_length, N_ROW, 2, FF // N_ROW)
    gate = gate_up[:, :, 0].reshape(sequence_length, FF)
    upward = gate_up[:, :, 1].reshape(sequence_length, FF)
    active = low(jax.nn.silu(gate) * upward)
    return middle + low_back(jnp.dot(active, down_full, precision=HIGHEST))

def arrange(values):
    shaped = values.reshape((N_DP, MB, SEQ_MB, SEG) + values.shape[1:])
    shaped = jnp.moveaxis(shaped, 0, 2)
    return shaped.reshape((MB * SEQ_MB, N_DP * SEG) + values.shape[1:])

def restore(values):
    shaped = values.reshape((MB, SEQ_MB, N_DP, SEG) + values.shape[2:])
    shaped = jnp.moveaxis(shaped, 2, 0)
    return shaped.reshape((N_DP * MB * SEQ_MB * SEG,) + values.shape[2:])

def reference(tokens, positions, prefix, norm1_gain, query_key_value_weight, out_weight, norm2_gain, gate_up_weight, down_weight, cotangent):
    seq_inputs = arrange(tokens.astype(jnp.float32))
    seq_places = arrange(positions)
    seq_cotangent = arrange(cotangent.astype(jnp.float32))
    weights = (norm1_gain.astype(jnp.float32), query_key_value_weight.astype(jnp.float32), out_weight.astype(jnp.float32), norm2_gain.astype(jnp.float32), gate_up_weight.astype(jnp.float32), down_weight.astype(jnp.float32))
    zeros = tuple((jnp.zeros_like(weight) for weight in weights))

    def one_sequence(totals, item):
        inputs, places, limit, upstream = item

        def apply(values, gain_one, qkv_full, out_full, gain_two, gate_up_full, down_full):
            return layer(values, gain_one, qkv_full, out_full, gain_two, gate_up_full, down_full, places, limit)
        result, pullback = jax.vjp(apply, inputs, weights[0], weights[1], weights[2], weights[3], weights[4], weights[5])
        grads = pullback(upstream)
        totals = tuple((total + grad for total, grad in zip(totals, grads[1:])))
        return (totals, (result, grads[0]))
    totals, (results, input_grads) = lax.scan(one_sequence, zeros, (seq_inputs, seq_places, prefix, seq_cotangent))
    output = restore(results).astype(jnp.bfloat16)
    input_grad = restore(input_grads)
    return (output, input_grad, totals[0], totals[1], totals[2], totals[3], totals[4], totals[5])
```

```python
import functools

import jax
import jax.numpy as jnp
from jax import lax
from jax.experimental import pallas as pl
from jax.experimental.pallas import tpu as pltpu
from jax.sharding import PartitionSpec as P

HEAD_SIZE = 64
SEG = 256
EPSILON = 1e-05
THETA = 10000.0
MASKED = -1e30
BF = jnp.bfloat16
F32 = jnp.float32


def nt(left, right):
    return lax.dot_general(left, right, (((1,), (1,)), ((), ())), preferred_element_type=F32)


def nn(left, right):
    return lax.dot_general(left, right, (((1,), (0,)), ((), ())), preferred_element_type=F32)


def tn(left, right):
    return lax.dot_general(left, right, (((0,), (0,)), ((), ())), preferred_element_type=F32)


def rope_tables(places):
    halfway = HEAD_SIZE // 2
    inverse = THETA ** (-(jnp.arange(halfway, dtype=F32) * 2.0 / HEAD_SIZE))
    angles = places.astype(F32)[:, None] * inverse[None, :]
    cosine, sine = jnp.cos(angles), jnp.sin(angles)
    return jnp.concatenate([cosine, cosine], -1), jnp.concatenate([sine, sine], -1)


def turned(values):
    halfway = HEAD_SIZE // 2
    return jnp.concatenate([-values[..., halfway:], values[..., :halfway]], axis=-1)


def rotate(values, cosine, sine):
    return values * cosine[:, None, :] + turned(values) * sine[:, None, :]


def unrotate(values, cosine, sine):
    return values * cosine[:, None, :] - turned(values * sine[:, None, :])


def block_mask(starts, bounds, segment, width):
    group = width // SEG
    bound = jnp.concatenate([bounds] * group, axis=1)
    place = starts[segment] + lax.broadcasted_iota(jnp.int32, (SEG, width), 0)
    return place < bound


def attend_kernel(segments, starts, bounds, q_ref, k_ref, v_ref, o_ref, log_ref, s_ref):
    q = q_ref[0]
    width = q.shape[0]
    scale = HEAD_SIZE ** (-0.5)
    highest = jnp.full((1, width), MASKED, F32)

    def score(j, highest):
        rows = pl.ds(pl.multiple_of(j * SEG, SEG), SEG)
        s = nt(k_ref[0, rows], q) * scale
        s = jnp.where(block_mask(starts, bounds[...], j, width), s, MASKED)
        s_ref[rows] = s
        return jnp.maximum(highest, jnp.max(s, axis=0, keepdims=True))

    highest = lax.fori_loop(0, segments, score, highest)

    def total(j, summed):
        rows = pl.ds(pl.multiple_of(j * SEG, SEG), SEG)
        p = jnp.exp(s_ref[rows] - highest)
        s_ref[rows] = p
        return summed + jnp.sum(p, axis=0, keepdims=True)

    summed = lax.fori_loop(0, segments, total, jnp.zeros((1, width), F32))
    inverse = 1.0 / summed

    def weigh(j, out):
        rows = pl.ds(pl.multiple_of(j * SEG, SEG), SEG)
        p = (s_ref[rows] * inverse).astype(BF)
        return out + tn(v_ref[0, rows], p)

    out = lax.fori_loop(0, segments, weigh, jnp.zeros((HEAD_SIZE, width), F32))
    o_ref[0] = out.T.astype(BF)
    log_ref[0] = highest + jnp.log(summed)


def attend_back_kernel(
    segments, starts, bounds, q_ref, k_ref, v_ref, do_ref, log_ref, delta_ref, dq_ref, dk_ref, dv_ref
):
    q, do = q_ref[0], do_ref[0]
    width = q.shape[0]
    scale = HEAD_SIZE ** (-0.5)
    logs, delta = log_ref[0], delta_ref[0]

    def visit(j, grad_q):
        rows = pl.ds(pl.multiple_of(j * SEG, SEG), SEG)
        k = k_ref[0, rows]
        s = nt(k, q) * scale
        s = jnp.where(block_mask(starts, bounds[...], j, width), s, MASKED)
        p = jnp.exp(s - logs)
        dp = nt(v_ref[0, rows], do)
        ds = (p * (dp - delta)).astype(BF)
        dk_ref[0, rows] = nn(ds, q) * scale
        dv_ref[0, rows] = nn(p.astype(BF), do)
        return grad_q + tn(k, ds)

    grad_q = lax.fori_loop(0, segments, visit, jnp.zeros((HEAD_SIZE, width), F32))
    dq_ref[0] = grad_q.T * scale


def head_spec(rows, last=HEAD_SIZE):
    return pl.BlockSpec((1, rows, last), lambda g, *_: (g, 0, 0))


def attend(starts, bounds, q, k, v):
    heads, width, _ = q.shape
    keys = k.shape[1]
    return pl.pallas_call(
        functools.partial(attend_kernel, keys // SEG),
        grid_spec=pltpu.PrefetchScalarGridSpec(
            num_scalar_prefetch=1,
            grid=(heads,),
            in_specs=[
                pl.BlockSpec((1, SEG), lambda g, *_: (0, 0)),
                head_spec(width),
                head_spec(keys),
                head_spec(keys),
            ],
            out_specs=[head_spec(width), head_spec(1, width)],
            scratch_shapes=[pltpu.VMEM((keys, width), F32)],
        ),
        out_shape=[
            jax.ShapeDtypeStruct(q.shape, BF),
            jax.ShapeDtypeStruct((heads, 1, width), F32),
        ],
        compiler_params=pltpu.CompilerParams(vmem_limit_bytes=60 << 20),
        name="attend",
    )(starts, bounds, q, k, v)


def attend_back(starts, bounds, q, k, v, do, logs, delta):
    heads, width, _ = q.shape
    keys = k.shape[1]
    return pl.pallas_call(
        functools.partial(attend_back_kernel, keys // SEG),
        grid_spec=pltpu.PrefetchScalarGridSpec(
            num_scalar_prefetch=1,
            grid=(heads,),
            in_specs=[
                pl.BlockSpec((1, SEG), lambda g, *_: (0, 0)),
                head_spec(width),
                head_spec(keys),
                head_spec(keys),
                head_spec(width),
                head_spec(1, width),
                head_spec(1, width),
            ],
            out_specs=[head_spec(width), head_spec(keys), head_spec(keys)],
        ),
        out_shape=[
            jax.ShapeDtypeStruct(q.shape, F32),
            jax.ShapeDtypeStruct(k.shape, F32),
            jax.ShapeDtypeStruct(k.shape, F32),
        ],
        compiler_params=pltpu.CompilerParams(vmem_limit_bytes=60 << 20),
        name="attend_back",
    )(starts, bounds, q, k, v, do, logs, delta)


def norm_forward(values):
    width = values.shape[1]
    scale = lax.rsqrt(jnp.sum(values * values, axis=1, keepdims=True) / width + EPSILON)
    return values * scale, scale


def norm_backward(normed, scale, gain, grad_normed):
    width = normed.shape[1]
    weighted = grad_normed * gain
    inner = jnp.sum(weighted * normed, axis=1, keepdims=True) / width
    return scale * (weighted - normed * inner), jnp.sum(grad_normed * normed, axis=0)


def shards(
    tokens,
    positions,
    prefix,
    norm1_gain,
    qkv_part,
    out_part,
    norm2_gain,
    gate_up_part,
    down_part,
    cotangent,
):
    rows_count, col_count, data_count = (lax.axis_size(a) for a in ("row", "col", "dp"))
    row, col, data = (lax.axis_index(a) for a in ("row", "col", "dp"))
    both = ("col", "dp")
    part = tokens.shape[1]
    width = part * col_count
    sequences = tokens.shape[0] // SEG
    per_row = sequences // rows_count
    assert per_row == col_count
    sequence = row * col_count + col
    query_heads = out_part.shape[0] // HEAD_SIZE
    kv_heads = (qkv_part.shape[1] // HEAD_SIZE - query_heads) // 2
    group = query_heads // kv_heads
    hidden = down_part.shape[0]

    gain_one = lax.all_gather(norm1_gain, both, axis=0, tiled=True).astype(F32)
    gain_two = lax.all_gather(norm2_gain, both, axis=0, tiled=True).astype(F32)
    qkv = lax.all_gather(qkv_part, ("row",) + both, axis=0, tiled=True)
    qkv = qkv.reshape(rows_count, width, qkv_part.shape[1])
    out_t = lax.all_gather(out_part.T, ("row",) + both, axis=0, tiled=True)
    out_t = out_t.reshape(rows_count, width, out_part.shape[0])
    gate_up = lax.all_gather(gate_up_part, both, axis=0, tiled=True)
    down_t = lax.all_gather(down_part.T, both, axis=0, tiled=True)

    mine = lax.dynamic_slice_in_dim(
        tokens.reshape(sequences, SEG, part), row * per_row, per_row, axis=0
    )
    mine = lax.all_to_all(mine, "col", 0, 0)
    x = mine.transpose(1, 0, 2).reshape(SEG, width).astype(F32)
    cot = lax.all_to_all(cotangent.reshape(rows_count, per_row, SEG, part), "col", 1, 1)
    cot = cot.transpose(0, 2, 1, 3).reshape(rows_count, SEG, width)
    cot_mine = lax.dynamic_index_in_dim(cot, row, 0, keepdims=False)
    cot_pair = cot.reshape(rows_count * SEG, width)

    starts_all = lax.all_gather(positions.reshape(sequences, SEG)[:, 0], "dp", axis=0)
    starts = lax.dynamic_index_in_dim(starts_all, sequence, 1, keepdims=False)
    limit = lax.dynamic_index_in_dim(prefix, sequence, 0, keepdims=False)
    places = lax.dynamic_index_in_dim(starts, data, 0, keepdims=False) + jnp.arange(
        SEG, dtype=jnp.int32
    )
    bounds = jnp.maximum(places + 1, limit)[None, :]
    cosine, sine = rope_tables(places)

    normed_one, scale_one = norm_forward(x)
    input_one = (normed_one * gain_one).astype(BF)
    queries, keys, values = [], [], []
    for r in range(rows_count):
        mixed = nn(input_one, qkv[r]).reshape(SEG, query_heads + 2 * kv_heads, HEAD_SIZE)
        queries.append(rotate(mixed[:, :query_heads], cosine, sine).astype(BF))
        keys.append(
            rotate(mixed[:, query_heads : query_heads + kv_heads], cosine, sine).astype(BF)
        )
        values.append(mixed[:, query_heads + kv_heads :].astype(BF))
    all_kv = rows_count * kv_heads
    q = jnp.concatenate(queries, 1).reshape(SEG, all_kv, group, HEAD_SIZE)
    q = q.transpose(1, 2, 0, 3).reshape(all_kv, group * SEG, HEAD_SIZE)
    kv = jnp.concatenate(keys + values, 1).reshape(SEG, 2 * all_kv * HEAD_SIZE)
    everyone = lax.all_gather(kv, "dp", axis=0, tiled=True)
    everyone = everyone.reshape(data_count * SEG, 2 * all_kv, HEAD_SIZE).transpose(1, 0, 2)
    k, v = everyone[:all_kv], everyone[all_kv:]
    heads, logs = attend(starts, bounds, q, k, v)
    heads_flat = heads.reshape(all_kv, group, SEG, HEAD_SIZE).transpose(2, 0, 1, 3)
    heads_flat = heads_flat.reshape(SEG, rows_count, query_heads * HEAD_SIZE)
    middle = x
    for r in range(rows_count):
        middle = middle + nt(heads_flat[:, r], out_t[r])
    normed_two, scale_two = norm_forward(middle)
    input_two = (normed_two * gain_two).astype(BF)

    pair = lax.all_gather(input_two, "row", axis=0, tiled=True)
    mix = nn(pair, gate_up)
    gate, upward = mix[:, :hidden], mix[:, hidden:]
    sigma = jax.nn.sigmoid(gate)
    active = (gate * sigma * upward).astype(BF)
    result = nt(active, down_t)
    result = middle + lax.psum_scatter(
        result.astype(BF), "row", scatter_dimension=0, tiled=True
    ).astype(F32)
    grad_down = tn(cot_pair, active)
    grad_active = nn(cot_pair, down_t)
    grad_gate = grad_active * upward * sigma * (1.0 + gate * (1.0 - sigma))
    grad_mix = jnp.concatenate([grad_gate, grad_active * gate * sigma], axis=1).astype(BF)
    grad_gate_up = tn(pair, grad_mix)
    grad_normed_two = lax.psum_scatter(
        nt(grad_mix, gate_up).astype(BF), "row", scatter_dimension=0, tiled=True
    ).astype(F32)
    back_two, grad_gain_two = norm_backward(normed_two, scale_two, gain_two, grad_normed_two)
    grad_middle = cot_mine.astype(F32) + back_two
    branch = grad_middle.astype(BF)
    grad_heads, grad_out = [], []
    for r in range(rows_count):
        grad_out.append(tn(branch, heads_flat[:, r]))
        grad_heads.append(nn(branch, out_t[r]).astype(BF))
    do = jnp.concatenate(grad_heads, 1).reshape(SEG, all_kv, group, HEAD_SIZE)
    do = do.transpose(1, 2, 0, 3).reshape(all_kv, group * SEG, HEAD_SIZE)
    delta = jnp.sum(do.astype(F32) * heads.astype(F32), axis=-1)[:, None, :]
    dq, dk, dv = attend_back(starts, bounds, q, k, v, do, logs, delta)
    dkv = jnp.concatenate([dk, dv], 0).transpose(1, 0, 2)
    dkv = dkv.reshape(data_count * SEG, 2 * all_kv * HEAD_SIZE).astype(BF)
    dkv = lax.psum_scatter(dkv, "dp", scatter_dimension=0, tiled=True).astype(F32)
    dkv = dkv.reshape(SEG, 2 * all_kv, HEAD_SIZE)
    dk, dv = unrotate(dkv[:, :all_kv], cosine, sine), dkv[:, all_kv:]
    dq = dq.reshape(all_kv, group, SEG, HEAD_SIZE).transpose(2, 0, 1, 3)
    dq = unrotate(dq.reshape(SEG, all_kv * group, HEAD_SIZE), cosine, sine)
    grad_qkv, grad_normed_one = [], 0.0
    for r in range(rows_count):
        ours = slice(r * kv_heads, (r + 1) * kv_heads)
        grad_mixed = jnp.concatenate(
            [dq[:, r * query_heads : (r + 1) * query_heads], dk[:, ours], dv[:, ours]], 1
        )
        grad_mixed = grad_mixed.reshape(SEG, qkv_part.shape[1]).astype(BF)
        grad_qkv.append(tn(input_one, grad_mixed))
        grad_normed_one = grad_normed_one + nt(grad_mixed, qkv[r])
    back_one, grad_gain_one = norm_backward(normed_one, scale_one, gain_one, grad_normed_one)
    grad_input = grad_middle + back_one

    def to_output(values):
        pieces = values.astype(BF).reshape(SEG, col_count, part).transpose(1, 0, 2)
        pieces = lax.all_to_all(pieces, "col", 0, 0)
        return lax.all_gather(pieces, "row", axis=0, tiled=True).reshape(sequences * SEG, part)

    def sum_half(parts):
        halves = lax.psum_scatter(
            jnp.stack(parts).astype(BF), "row", scatter_dimension=0, tiled=True
        )
        halves = halves.reshape(halves.shape[1:])
        return lax.psum_scatter(halves, both, scatter_dimension=0, tiled=True).astype(F32)

    def sum_whole(values):
        return lax.psum_scatter(values.astype(BF), both, scatter_dimension=0, tiled=True).astype(
            F32
        )

    gains = lax.psum(jnp.stack([grad_gain_one, grad_gain_two]), ("row",) + both)
    gains = lax.dynamic_slice_in_dim(
        gains, (col * data_count + data) * norm1_gain.shape[0], norm1_gain.shape[0], axis=1
    )
    return (
        to_output(result),
        to_output(grad_input).astype(F32),
        gains[0],
        sum_half(grad_qkv),
        sum_half(grad_out).T,
        gains[1],
        sum_whole(grad_gate_up),
        sum_whole(grad_down).T,
    )


def solution(mesh):
    both = ("col", "dp")
    in_specs = (
        P("dp", "col"),
        P("dp"),
        P(),
        P(both),
        P(both, "row"),
        P("row", both),
        P(both),
        P(both, "row"),
        P("row", both),
        P("dp", "col"),
    )
    out_specs = (
        P("dp", "col"),
        P("dp", "col"),
        P(both),
        P(both, "row"),
        P("row", both),
        P(both),
        P(both, "row"),
        P("row", both),
    )
    return jax.shard_map(shards, mesh=mesh, in_specs=in_specs, out_specs=out_specs, check_vma=False)
```
